32 devices in a mesh: dp: 8 (over z, y), tensor: 4 (over x, core).
Axes of the slice: x: 2, y: 2, z: 4, core: 2. Of those that a mesh axis runs over, the one named last changes fastest.
Arguments:
- face_grads: bfloat16 [2048, 2048], P('dp', 'tensor'), may hold values from -6 to 6
- face_owner: int32 [2048, 1], P('dp'), may hold values from 0 to 7; in each aligned block of 256 rows (0 to 255, 256 to 511, ...) at most 64 rows name the same one
- face_slot: int32 [2048, 1], P('dp'), may hold values from 0 to 255
- queries: bfloat16 [2048, 1024], P('dp', 'tensor'), may hold values from -6 to 6
- context_keys: bfloat16 [512, 1024], P(None, 'tensor'), may hold values from -6 to 6
- context_values: bfloat16 [512, 1024], P(None, 'tensor'), may hold values from -6 to 6
- w_out: bfloat16 [1024, 2048], P('tensor'), may hold values from -0.1875 to 0.1875
- branch_gate: float32 [2048], replicated, may hold values from 0.3 to 3
Outputs:
- grad_q: bfloat16 [2048, 1024], P('dp', 'tensor')
- grad_wo_t: float32 [2048, 1024], P('dp', 'tensor')
- grad_k: float32 [512, 1024], P('dp', 'tensor')
- grad_v: float32 [512, 1024], P('dp', 'tensor')
The draws below stay inside these ranges and needn't reach their ends.
Inputs may be any that keep to these rules, and one draw needn't show every extreme that they name: `face_owner`: at most 64 of the 256 face rows of one dp index name the same owner.
All inputs are finite; a program needn't handle non-finite values.
Results may differ from the reference program's by a relative error of at most 0.03.
Values may be sent and summed in bfloat16 or wider, within the bound.
No kernel may reach another device: no remote copies, remote signals or barrier semaphores. Data moves between devices by JAX's collectives and lax.ppermute only.
A program may use at most 64 MiB of HBM per device.

```python
import math
import jax
import jax.numpy as jnp
import numpy as np
from jax import lax

D = 2048
HEADS = 8
HD = 128
CTX = 512
TOK_DEV = 256
FACE_DEV = 256
CAP = 64
TOKENS = 2048
FACES = 2048
N_DP = 8


def draw_context_keys(key, part):
    normal_part = jnp.clip(jax.random.normal(jax.random.fold_in(key, 3), (CTX, HEADS, HD), jnp.float32), -6.0, 6.0)
    return normal_part.reshape(CTX, HEADS * HD).astype(jnp.bfloat16)


def draw_queries(key, part):
    normal_part = jnp.clip(jax.random.normal(jax.random.fold_in(key, 5), (TOKENS, HEADS, HD), jnp.float32), -6.0, 6.0)
    return normal_part.reshape(TOKENS, HEADS * HD).astype(jnp.bfloat16)


def touch_ends(values, own_key, low, top_value):
    spot = [jax.random.randint(jax.random.fold_in(own_key, axis), (), 0, length) for axis, length in enumerate(values.shape)]
    longest = values.shape.index(max(values.shape))
    beside = spot[:longest] + [(spot[longest] + 1) % values.shape[longest]] + spot[longest + 1:]
    return values.at[tuple(spot)].set(low).at[tuple(beside)].set(top_value)


def shard_levels(key, shape, pieces, smallest, top_value):
    def one(position, shards_of):
        heights = jax.random.uniform(jax.random.fold_in(jax.random.fold_in(key, 6), position), (shards_of,), jnp.float32, smallest / len(pieces), top_value / len(pieces))
        return jnp.repeat(jnp.exp(heights), shape[position] // shards_of).reshape((-1,) + (1,) * (len(shape) - position - 1))

    level = one(*pieces[0])
    for cut in pieces[1:]:
        level = level * one(*cut)
    return level


def routed_block(key, own, number, rows, count, top, most, slope):
    ranking = jax.random.permutation(key, count)
    heavy_load, usual = load_shares(count, rows * top, most, slope, True), load_shares(count, rows * top, most, slope, False)
    places = jnp.arange(count)

    def named(sizes, turn):
        used = int((sizes > 0).sum())
        fixed = max(1, used // 4)
        shifted = fixed + (places - fixed + turn * (used - fixed)) % max(1, count - fixed)
        return jnp.zeros((count,), jnp.int32).at[ranking[jnp.where(places < fixed, places, shifted)]].set(jnp.asarray(sizes, jnp.int32))

    sizes = jnp.where(number % 4 == 0, named(heavy_load, number // 4), named(usual, number - number // 4 - 1))
    mixed = jax.random.permutation(jax.random.fold_in(own, 3), count)
    giver, taker = mixed[0:count // 2 * 2:2], mixed[1:count // 2 * 2:2]
    margin = jnp.minimum(sizes[giver] - 1, most - sizes[taker]) // 2
    margin = jnp.where((giver == ranking[0]) | (taker == ranking[0]) | (sizes[taker] == 0), 0, jnp.maximum(margin, 0))
    shifted = jax.random.randint(jax.random.fold_in(own, 4), (count // 2,), 0, 1 << 20) % (margin + 1)
    sizes = sizes.at[giver].add(-shifted).at[taker].add(shifted)
    items = jnp.searchsorted(jnp.cumsum(sizes), jnp.arange(rows * top), side="right").astype(jnp.int32)
    table = items.reshape(top, rows).T
    table = table[jax.random.permutation(jax.random.fold_in(own, 1), rows)]
    turn = jax.random.randint(jax.random.fold_in(own, 2), (rows, 1), 0, top)
    return jnp.take_along_axis(table, (jnp.arange(top)[None, :] + turn) % top, axis=1)


def load_shares(number_of, total, most, slope, full):
    portions = [(1 << 20) // math.isqrt(grade ** slope) + 1 for grade in range(1, number_of + 1)]
    largest = most if full else min(most, max(-(-total // number_of), total * portions[0] // sum(portions)))
    least = 1 if total - largest >= number_of - 1 else 0
    given, rest = [largest] + [least] * (number_of - 1), total - largest - least * (number_of - 1)
    while rest > 0:
        candidates = [i for i in range(1, number_of) if given[i] < largest] or [i for i in range(1, number_of) if given[i] < most]
        mass, left = sum([portions[i] for i in candidates]), rest
        for i in candidates:
            extra = min(most - given[i], max(1, left * portions[i] // mass), rest)
            given[i] = given[i] + extra
            rest = rest - extra
    return np.array(given)


def bell_draw(own_key, extent, width, most, shards=(), kind=jnp.bfloat16):
    factor_of = shard_levels(own_key, extent, shards, -0.22, 0.18) if shards else 1.0
    result = jax.random.normal(own_key, extent, jnp.float32) * width * factor_of
    return jnp.minimum(jnp.maximum(result, -most), most).astype(kind)


def setup_inputs(seed: int = 0) -> dict:
    arg_keys = jax.random.split(jax.random.key(seed), 9)
    face_grads = bell_draw(arg_keys[0], (FACES, D), 1.0, 6.0, ((0, 8), (1, 4)))
    face_owner_keys = jax.random.split(jax.random.fold_in(arg_keys[1], 1), FACES // FACE_DEV)
    face_owner_turns = jax.random.permutation(jax.random.fold_in(arg_keys[1], 3), FACES // FACE_DEV)
    face_owner = jax.vmap(lambda own, number: routed_block(jax.random.fold_in(arg_keys[1], 2), own, number, FACE_DEV, N_DP, 1, CAP, 2))(face_owner_keys, face_owner_turns).reshape((FACES, 1))
    face_slot = touch_ends(jax.random.randint(arg_keys[2], (FACES, 1), 0, TOK_DEV), jax.random.fold_in(arg_keys[2], 1), 0, TOK_DEV - 1).astype(jnp.int32)
    queries = draw_queries(jax.random.fold_in(arg_keys[8], 71), 0)
    context_keys = draw_context_keys(jax.random.fold_in(arg_keys[8], 71), 0)
    context_values = bell_draw(arg_keys[5], (CTX, HEADS * HD), 1.0, 6.0, ((1, 4),))
    w_out = bell_draw(arg_keys[6], (HEADS * HD, D), (HEADS * HD) ** -0.5, 0.1875, ((0, 4),))
    branch_gate = jnp.clip(jnp.exp(jax.random.uniform(arg_keys[7], (D,), jnp.float32, math.log(0.3), math.log(3.0))), 0.3, 3.0)
    return dict(face_grads=face_grads, face_owner=face_owner, face_slot=face_slot, queries=queries, context_keys=context_keys, context_values=context_values, w_out=w_out, branch_gate=branch_gate)


def reference(face_grads, face_owner, face_slot, queries, context_keys, context_values, w_out, branch_gate):
    token_index = (face_owner[:, 0] * TOK_DEV + face_slot[:, 0]).astype(jnp.int32)
    grad_out = jax.ops.segment_sum(face_grads.astype(jnp.float32), token_index, num_segments=TOKENS).astype(jnp.bfloat16)
    branch_grad = (branch_gate[None, :] * grad_out.astype(jnp.float32)).astype(jnp.bfloat16)
    grad_attn = jnp.dot(branch_grad, w_out.T, preferred_element_type=jnp.float32).astype(jnp.bfloat16)
    score_scale = 1.0 / math.sqrt(HD)
    keys_f = context_keys.astype(jnp.float32).reshape(CTX, HEADS, HD)
    values_f = context_values.astype(jnp.float32).reshape(CTX, HEADS, HD)
    block_rows = math.gcd(TOKENS, 4096)
    block_total = TOKENS // block_rows

    def block_step(totals, block_index):
        first_row = (block_index * block_rows).astype(jnp.int32)
        query_block = lax.dynamic_slice_in_dim(queries, first_row, block_rows, 0).astype(jnp.float32).reshape(block_rows, HEADS, HD)
        attn_grad_bf = lax.dynamic_slice_in_dim(grad_attn, first_row, block_rows, 0)
        attn_grad = attn_grad_bf.astype(jnp.float32).reshape(block_rows, HEADS, HD)
        branch_block = lax.dynamic_slice_in_dim(branch_grad, first_row, block_rows, 0)
        scores = jnp.einsum('thd,chd->htc', query_block, keys_f) * score_scale
        weights = jax.nn.softmax(scores, axis=-1)
        probs_bf = lax.optimization_barrier(weights.astype(jnp.bfloat16))
        probs_f = probs_bf.astype(jnp.float32)
        attention = jnp.einsum('htc,chd->thd', probs_f, values_f).astype(jnp.bfloat16).reshape(block_rows, HEADS * HD)
        wo_term = jnp.dot(branch_block.T, attention, preferred_element_type=jnp.float32)
        grad_probs = jnp.einsum('thd,chd->htc', attn_grad, values_f)
        row_delta = lax.optimization_barrier(jnp.sum(weights * grad_probs, axis=-1, keepdims=True))
        score_bf = lax.optimization_barrier((weights * (grad_probs - row_delta)).astype(jnp.bfloat16))
        score_grad = score_bf.astype(jnp.float32)
        query_grad = (score_scale * jnp.einsum('htc,chd->thd', score_grad, keys_f)).astype(jnp.bfloat16).reshape(block_rows, HEADS * HD)
        key_term = score_scale * jnp.einsum('htc,thd->chd', score_grad, query_block)
        value_term = jnp.einsum('htc,thd->chd', probs_f, attn_grad)
        new_totals = (totals[0] + wo_term, totals[1] + key_term.reshape(CTX, HEADS * HD), totals[2] + value_term.reshape(CTX, HEADS * HD))
        return (new_totals, query_grad)
    start_totals = (jnp.zeros((D, HEADS * HD), jnp.float32), jnp.zeros((CTX, HEADS * HD), jnp.float32), jnp.zeros((CTX, HEADS * HD), jnp.float32))
    totals, query_blocks = lax.scan(block_step, start_totals, jnp.arange(block_total, dtype=jnp.int32))
    grad_q = query_blocks.reshape(TOKENS, HEADS * HD)
    return (grad_q, totals[0], totals[1], totals[2])
```

```python
import functools
import math

import jax
import jax.numpy as jnp
from jax import lax
from jax.experimental import pallas as pl
from jax.experimental.pallas import tpu as pltpu
from jax.sharding import PartitionSpec as P

HD = 128
F32 = jnp.float32
BF16 = jnp.bfloat16


def route_rows(face_block, face_owner, face_slot, num_dp, tok_rows):
    face_rows = face_block.shape[0]
    capacity = 2 * face_rows // num_dp
    owner_index = face_owner[:, 0]
    marker = (owner_index[:, None] == jnp.arange(num_dp, dtype=jnp.int32)[None, :]).astype(
        jnp.int32
    )
    earlier = jnp.cumsum(marker, axis=0) - marker
    in_bucket = jnp.sum(earlier * marker, axis=1)
    places = owner_index * capacity + in_bucket
    outgoing = (
        jnp.zeros((num_dp * capacity, face_block.shape[1]), face_block.dtype)
        .at[places]
        .set(face_block)
    )
    targets = jnp.full((num_dp * capacity,), tok_rows, jnp.int32).at[places].set(face_slot[:, 0])
    return (
        outgoing.reshape(num_dp, capacity, face_block.shape[1]),
        targets.reshape(num_dp, capacity),
    )


def land_rows(arrived, landed, tok_rows):
    row_width = arrived.shape[2]
    summed = jax.ops.segment_sum(
        arrived.reshape(-1, row_width).astype(jnp.float32),
        landed.reshape(-1),
        num_segments=tok_rows + 1,
    )
    return summed[:tok_rows].astype(jnp.bfloat16)


def routed_body(
    face_grads, face_owner, face_slot, queries, context_keys, context_values, w_out, branch_gate
):
    num_dp = lax.axis_size("dp")
    tok_rows = queries.shape[0]
    outgoing, targets = route_rows(face_grads, face_owner, face_slot, num_dp, tok_rows)
    arrived, landed = (
        lax.all_to_all(outgoing, "dp", split_axis=0, concat_axis=0, tiled=True),
        lax.all_to_all(targets, "dp", split_axis=0, concat_axis=0, tiled=True),
    )
    partial_out = land_rows(arrived, landed, tok_rows)
    grad_out = lax.all_gather(partial_out, "tensor", axis=1, tiled=True)
    branch_grad = (branch_gate[None, :] * grad_out.astype(jnp.float32)).astype(jnp.bfloat16)
    grad_attn = lax.dot_general(
        branch_grad, w_out, (((1,), (1,)), ((), ())), preferred_element_type=jnp.float32
    ).astype(jnp.bfloat16)
    local_heads = queries.shape[1] // HD
    context_rows = context_keys.shape[0]
    score_scale = 1.0 / math.sqrt(HD)
    query_heads = queries.reshape(tok_rows, local_heads, HD)
    key_heads = context_keys.reshape(context_rows, local_heads, HD)
    value_heads = context_values.reshape(context_rows, local_heads, HD)
    attn_grad = grad_attn.reshape(tok_rows, local_heads, HD)
    scores = (
        jnp.einsum("thd,chd->htc", query_heads, key_heads, preferred_element_type=jnp.float32)
        * score_scale
    )
    weights = jax.nn.softmax(scores, axis=-1)
    probs = weights.astype(jnp.bfloat16)
    attention = (
        jnp.einsum("htc,chd->thd", probs, value_heads, preferred_element_type=jnp.float32)
        .astype(jnp.bfloat16)
        .reshape(tok_rows, local_heads * HD)
    )
    grad_probs = jnp.einsum(
        "thd,chd->htc", attn_grad, value_heads, preferred_element_type=jnp.float32
    )
    row_delta = jnp.sum(weights * grad_probs, axis=-1, keepdims=True)
    score_grad = (weights * (grad_probs - row_delta)).astype(jnp.bfloat16)
    grad_q = (
        (
            score_scale
            * jnp.einsum("htc,chd->thd", score_grad, key_heads, preferred_element_type=jnp.float32)
        )
        .astype(jnp.bfloat16)
        .reshape(tok_rows, local_heads * HD)
    )
    key_term = score_scale * jnp.einsum(
        "htc,thd->chd", score_grad, query_heads, preferred_element_type=jnp.float32
    )
    value_term = jnp.einsum("htc,thd->chd", probs, attn_grad, preferred_element_type=jnp.float32)
    grad_k, grad_v = (
        lax.psum_scatter(
            key_term.reshape(context_rows, local_heads * HD), "dp", scatter_dimension=0, tiled=True
        ),
        lax.psum_scatter(
            value_term.reshape(context_rows, local_heads * HD),
            "dp",
            scatter_dimension=0,
            tiled=True,
        ),
    )
    grad_wo_t = lax.psum_scatter(
        lax.dot_general(
            branch_grad, attention, (((0,), (0,)), ((), ())), preferred_element_type=jnp.float32
        ),
        "dp",
        scatter_dimension=0,
        tiled=True,
    )
    return (grad_q, grad_wo_t, grad_k, grad_v)


NN = (((1,), (0,)), ((), ()))
NT = (((1,), (1,)), ((), ()))
TN = (((0,), (0,)), ((), ()))


def dot(a, b, dims):
    return lax.dot_general(a, b, dims, preferred_element_type=F32)


def kernel_call(body, outs, args, flops, scratch=()):
    nbytes = sum(a.size * a.dtype.itemsize for a in args) + sum(
        math.prod(o.shape) * o.dtype.itemsize for o in outs
    )
    vmem = pl.BlockSpec(memory_space=pltpu.VMEM)
    return pl.pallas_call(
        body,
        out_shape=tuple(outs),
        in_specs=[vmem] * len(args),
        out_specs=tuple([vmem] * len(outs)),
        scratch_shapes=list(scratch),
        cost_estimate=pl.CostEstimate(flops=flops, bytes_accessed=nbytes, transcendentals=0),
        compiler_params=pltpu.CompilerParams(vmem_limit_bytes=48 * 2**20),
        name=body.func.__name__ if isinstance(body, functools.partial) else body.__name__,
    )(*args)


def half_columns(ref, half, width):
    return ref[:, pl.ds(pl.multiple_of(half * width, width), width)]


def early_halves(f0_ref, f1_ref, out_ref):
    other = 1 - lax.axis_index("dp") % 2
    rows, width = f0_ref.shape[0], f0_ref.shape[1] // 2
    out_ref[0:rows, :] = half_columns(f0_ref, other, width)
    out_ref[rows : 2 * rows, :] = half_columns(f1_ref, other, width)


def face_attn(tensor_bits, *refs):
    n = len(tensor_bits)
    faces, wg_ref, ga_ref, late_ref = refs[:n], refs[n], refs[n + 1], refs[n + 2]
    other = 1 - lax.axis_index("dp") % 2
    me = lax.axis_index("tensor")
    rows, width = faces[0].shape
    total = None
    for bits, f_ref in zip(tensor_bits, faces):
        block = me ^ bits
        term = dot(f_ref[...], half_columns(wg_ref, block, width), NT)
        total = term if total is None else total + term
    ga_ref[...] = total.astype(BF16)
    for k, f_ref in enumerate(faces[n // 2 :]):
        late_ref[k * rows : (k + 1) * rows, :] = half_columns(f_ref, other, width // 2)


def token_match(tok_ref, first, count):
    faces = tok_ref.shape[1]
    rows = lax.broadcasted_iota(jnp.int32, (count, faces), 0) + first
    return jnp.where(rows == tok_ref[...], 1.0, 0.0).astype(BF16)


def gather_queries(tok_own, tok_other, *refs):
    qs, out_ref = refs[:-1], refs[-1]
    here = lax.axis_index("dp")
    z, y = here // 2, here % 2
    tokens = qs[0].shape[0]
    faces = tok_own.shape[1]
    for part, tok in enumerate((tok_own, tok_other)):
        total = None
        for k, q_ref in enumerate(qs):
            owner = (z ^ k) * 2 + y
            term = dot(token_match(tok, owner * tokens, tokens), q_ref[...], TN)
            total = term if total is None else total + term
        out_ref[part * faces : (part + 1) * faces, :] = total.astype(BF16)


def scatter_grads(tok_own, tok_other, ga_own, ga_other, *outs):
    here = lax.axis_index("dp")
    z, y = here // 2, here % 2
    tokens = outs[0].shape[0]
    for k, out_ref in enumerate(outs):
        owner = (z ^ k) * 2 + y
        total = dot(token_match(tok_own, owner * tokens, tokens), ga_own[...], NN) + dot(
            token_match(tok_other, owner * tokens, tokens), ga_other[...], NN
        )
        out_ref[...] = total.astype(out_ref.dtype)


def softmax_rows(q, k, scale):
    s = dot(q, k, NT) * scale
    e = jnp.exp(s - jnp.max(s, axis=-1, keepdims=True))
    return e / jnp.sum(e, axis=-1, keepdims=True)


def face_partials(tensor_bits, *refs):
    n = len(tensor_bits)
    faces = refs[:n]
    early_ref, late_ref, q_mine, q_got, ga_own, ga_other, k_ref, v_ref = refs[n : n + 8]
    outs = refs[n + 8 : -3]
    wo_s, gk_s, gv_s = refs[-3:]
    here = lax.axis_index("dp")
    me = lax.axis_index("tensor")
    z, y = here // 2, here % 2
    rows, width = faces[0].shape
    half = width // 2
    scale = 1.0 / math.sqrt(HD)
    heads = k_ref.shape[1] // HD
    att = []
    for part in range(2):
        mine, got = part * rows, (1 - part) * rows
        q_all = q_mine[mine : mine + rows, :] + q_got[got : got + rows, :]
        ga_all = (ga_own, ga_other)[part][...]
        att_heads = []
        for h in range(heads):
            cols = slice(h * HD, (h + 1) * HD)
            q, ga, k, v = q_all[:, cols], ga_all[:, cols], k_ref[:, cols], v_ref[:, cols]
            weights = softmax_rows(q, k, scale)
            probs = weights.astype(BF16)
            att_heads.append(dot(probs, v, NN).astype(BF16))
            gp = dot(ga, v, NT)
            delta = jnp.sum(weights * gp, axis=-1, keepdims=True)
            sg = (weights * (gp - delta)).astype(BF16)
            gk = dot(sg, q, TN) * scale
            gv = dot(probs, ga, TN)
            if part == 0:
                gk_s[:, cols] = gk
                gv_s[:, cols] = gv
            else:
                gk_s[:, cols] += gk
                gv_s[:, cols] += gv
        att.append(jnp.concatenate(att_heads, axis=1))
    for m, bits in enumerate(tensor_bits):
        other_ref = early_ref if m < n // 2 else late_ref
        at = (m % (n // 2)) * rows
        wo = dot(half_columns(faces[m], y, half), att[0], TN) + dot(
            other_ref[at : at + rows, :], att[1], TN
        )
        wo_s[me ^ bits] = wo
    ctx = k_ref.shape[0] // (2 * n)
    for k, out_ref in enumerate(outs):
        to = z ^ k
        at = pl.ds(pl.multiple_of((to * 2 + y) * ctx, ctx), ctx)
        out_ref[0:half, :] = wo_s[to].astype(out_ref.dtype)
        out_ref[half : half + ctx, :] = gk_s[at, :].astype(out_ref.dtype)
        out_ref[half + ctx : half + 2 * ctx, :] = gv_s[at, :].astype(out_ref.dtype)


def query_grads(q_ref, k_ref, v_ref, *refs):
    gs, out_ref = refs[:-1], refs[-1]
    scale = 1.0 / math.sqrt(HD)
    total = gs[0][...].astype(F32)
    for g in gs[1:]:
        total = total + g[...].astype(F32)
    ga_all = total.astype(BF16)
    for h in range(k_ref.shape[1] // HD):
        cols = slice(h * HD, (h + 1) * HD)
        q, k, v, ga = q_ref[:, cols], k_ref[:, cols], v_ref[:, cols], ga_all[:, cols]
        weights = softmax_rows(q, k, scale)
        gp = dot(ga, v, NT)
        delta = jnp.sum(weights * gp, axis=-1, keepdims=True)
        sg = (weights * (gp - delta)).astype(BF16)
        out_ref[:, cols] = (dot(sg, k, NN) * scale).astype(BF16)


def final_sums(gate_ref, *refs):
    parts = refs[:-3]
    wo_ref, gk_ref, gv_ref = refs[-3:]
    here = lax.axis_index("dp")
    rows, ctx = wo_ref.shape[0], gk_ref.shape[0]
    gate_row = gate_ref[pl.ds(here, 1), :]
    diag = lax.broadcasted_iota(jnp.int32, (rows, rows), 0) == lax.broadcasted_iota(
        jnp.int32, (rows, rows), 1
    )
    gate_col = jnp.sum(jnp.where(diag, gate_row, 0.0), axis=1, keepdims=True)
    total = parts[0][...].astype(F32)
    for p in parts[1:]:
        total = total + p[...].astype(F32)
    wo_ref[...] = total[0:rows, :] * gate_col
    gk_ref[...] = total[rows : rows + ctx, :]
    gv_ref[...] = total[rows + ctx : rows + 2 * ctx, :]


def face_body(
    face_grads, face_owner, face_slot, queries, context_keys, context_values, w_out, branch_gate
):
    n_dp, n_tensor = lax.axis_size("dp"), lax.axis_size("tensor")
    a = n_dp // 2
    tokens, cols = queries.shape
    faces, width = face_grads.shape
    ctx = context_keys.shape[0]
    d = w_out.shape[1]

    def swap(x, axis, size, bits):
        return lax.ppermute(x, axis, [(i, i ^ bits) for i in range(size)])

    over_z = lambda x, k: swap(x, "dp", n_dp, 2 * k)
    over_y = lambda x: swap(x, "dp", n_dp, 1)
    over_t = lambda x, bits: swap(x, "tensor", n_tensor, bits)

    bits, blocks = [0], [face_grads]
    high = n_tensor // 2
    far = over_t(face_grads, high)
    near = [face_grads]
    near_bits = [0]
    step = 1
    while step < high:
        near = near + [over_t(x, step) for x in near]
        near_bits = near_bits + [b ^ step for b in near_bits]
        step *= 2
    away = [far]
    step = 1
    while step < high:
        away = away + [over_t(x, step) for x in away]
        step *= 2
    blocks = near + away
    bits = near_bits + [b ^ high for b in near_bits]

    tok = (face_owner * tokens + face_slot).reshape(1, faces)
    tok_other = over_y(tok)
    q_all = [queries] + [over_z(queries, k) for k in range(1, a)]
    wg = (w_out.astype(F32) * branch_gate[None, :]).astype(BF16)

    bf = lambda *s: jax.ShapeDtypeStruct(s, BF16)
    (early,) = kernel_call(
        early_halves, [bf(len(near) * faces, width // 2)], near, flops=0
    )
    early_got = over_y(early)
    ga, late = kernel_call(
        functools.partial(face_attn, bits),
        [bf(faces, cols), bf(len(away) * faces, width // 2)],
        blocks + [wg],
        flops=2 * faces * cols * d,
    )
    ga_other = over_y(ga)
    late_got = over_y(late)
    (q_part,) = kernel_call(
        gather_queries,
        [bf(2 * faces, cols)],
        [tok, tok_other] + q_all,
        flops=4 * faces * tokens * a * cols,
    )
    q_got = over_y(q_part)
    grads = kernel_call(
        scatter_grads,
        [bf(tokens, cols)] * a,
        [tok, tok_other, ga, ga_other],
        flops=4 * faces * tokens * a * cols,
    )
    grads_got = [grads[0]] + [over_z(g, k) for k, g in enumerate(grads) if k]

    out_rows = width // 2 + 2 * (ctx // n_dp)
    parts = kernel_call(
        functools.partial(face_partials, bits),
        [jax.ShapeDtypeStruct((out_rows, cols), F32)] + [bf(out_rows, cols)] * (a - 1),
        blocks
        + [early_got, late_got, q_part, q_got, ga, ga_other, context_keys, context_values],
        flops=20 * faces * ctx * cols + 2 * faces * d * cols,
        scratch=[
            pltpu.VMEM((a, width // 2, cols), F32),
            pltpu.VMEM((ctx, cols), F32),
            pltpu.VMEM((ctx, cols), F32),
        ],
    )
    parts_got = [parts[0]] + [over_z(p, k) for k, p in enumerate(parts) if k]
    (grad_q,) = kernel_call(
        query_grads,
        [bf(tokens, cols)],
        [queries, context_keys, context_values] + grads_got,
        flops=6 * tokens * ctx * cols,
    )
    gate_rows = branch_gate.reshape(n_dp, d // n_dp)
    f32 = lambda *s: jax.ShapeDtypeStruct(s, F32)
    grad_wo_t, grad_k, grad_v = kernel_call(
        final_sums,
        [f32(width // 2, cols), f32(ctx // n_dp, cols), f32(ctx // n_dp, cols)],
        [gate_rows] + parts_got,
        flops=0,
    )
    return grad_q, grad_wo_t, grad_k, grad_v


def solution(mesh):
    n_dp, n_tensor = mesh.shape["dp"], mesh.shape["tensor"]
    paired = n_dp == 2 * n_tensor and n_tensor & (n_tensor - 1) == 0 and n_tensor > 1
    in_specs = (
        P("dp", "tensor"),
        P("dp", None),
        P("dp", None),
        P("dp", "tensor"),
        P(None, "tensor"),
        P(None, "tensor"),
        P("tensor", None),
        P(),
    )
    out_specs = (P("dp", "tensor"), P("dp", "tensor"), P("dp", "tensor"), P("dp", "tensor"))
    body = face_body if paired else routed_body
    return jax.shard_map(body, mesh=mesh, in_specs=in_specs, out_specs=out_specs, check_vma=False)
```
